128 devices in a mesh: fsdp: 4 (over x_hi, core), ctx: 32 (over y, z, x_lo).
Axes of the slice: x: 4 (x_hi: 2, x_lo: 2; x = x_hi * 2 + x_lo), y: 4, z: 4, core: 2. Of those that a mesh axis runs over, the one named last changes fastest.
Arguments:
- query_branch: bfloat16 [4, 8192, 4096], P('fsdp', 'ctx'), may hold values from -6 to 6
- key_branch: bfloat16 [4, 8192, 4096], P('fsdp', 'ctx'), may hold values from -6 to 6
- value_branch: bfloat16 [4, 8192, 4096], P('fsdp', 'ctx'), may hold values from -6 to 6
- cotangent: bfloat16 [4, 8192, 4096], P('fsdp', 'ctx'), may hold values from -6 to 6
- quantized_weight_codes: int32 [4096, 4096], P('ctx', 'fsdp'), may hold values from 0 to 15
- scale_code_bytes: int32 [4096, 64], P('ctx', 'fsdp'), may hold values from 0 to 255
- row_scale_second: float32 [4096], P('ctx'), may hold values from 0.01 to 0.1
- filters: bfloat16 [256, 128], replicated, may hold values from -0.5 to 0.5
- channel_skip_weight: float32 [4096], replicated, may hold values from -6 to 6
- adapter_down_weight: bfloat16 [4096, 64], P('ctx'), may hold values from -0.09375 to 0.09375
- adapter_up_weight: bfloat16 [64, 4096], P(None, 'fsdp'), may hold values from -0.75 to 0.75
Outputs:
- output: bfloat16 [4, 8192, 4096], P('fsdp', 'ctx')
- grad_query: bfloat16 [4, 8192, 4096], P('fsdp', 'ctx')
- grad_key: bfloat16 [4, 8192, 4096], P('fsdp', 'ctx')
- grad_value: bfloat16 [4, 8192, 4096], P('fsdp', 'ctx')
- grad_down: bfloat16 [4096, 64], P('ctx')
- grad_up: bfloat16 [64, 4096], P(None, 'fsdp')
The draws below stay inside these ranges and needn't reach their ends.
All inputs are finite; a program needn't handle non-finite values.
Results may differ from the reference program's by a relative error of at most 0.0067.
Values may be sent and summed in bfloat16 or wider, within the bound.
No kernel may reach another device: no remote copies, remote signals or barrier semaphores. Data moves between devices by JAX's collectives and lax.ppermute only.
A program may use at most 256 MiB of HBM per device.

```python
import math
import jax
import jax.numpy as jnp

OPERATOR_WIDTH = 4096
OUTPUT_FEATURES = 4096
FL = 128
ADAPTER_RANK = 64
QBLOCK = 64
SEQS = 4
SEQLEN = 8192
GROUPS = 256
SCALE_COLS = 64


def touch_ends(drawn, rng, least, top_value):
    longest = drawn.shape.index(max(drawn.shape))
    spots = []
    for shift in (0, 1):
        where = [jax.random.randint(jax.random.fold_in(rng, axis), (), 0, length) for axis, length in enumerate(drawn.shape)]
        where[longest] = (where[longest] + shift) % drawn.shape[longest]
        spots.append(tuple(where))
    return drawn.at[spots[0]].set(least).at[spots[1]].set(top_value)


def raised(entries, key, source, target, blocks, factor):
    owner, partner = [(jnp.arange(entries.shape[position]) // (entries.shape[position] // blocks)).reshape([-1 if axis == position else 1 for axis in range(entries.ndim)]) for position in (source, target)]
    chosen = jax.random.permutation(key, blocks)[partner]
    strong = (owner == chosen) | (owner == (partner + blocks // 2) % blocks)
    return jnp.where(strong, factor * entries, entries)


def block_levels(key, extent, split, low, largest):
    loudness = 1.0
    for axis_at, shards_of in split:
        steps = jax.random.uniform(jax.random.fold_in(jax.random.fold_in(key, 6), axis_at), (shards_of,), jnp.float32, low / len(split), largest / len(split))
        loudness = loudness * jnp.repeat(jnp.exp(steps), extent[axis_at] // shards_of).reshape((-1,) + (1,) * (len(extent) - 1 - axis_at))
    return loudness


def normal_values(rng, shape, spread, limit, cuts=(), kind=jnp.bfloat16):
    level = block_levels(rng, shape, cuts, -0.22, 0.18) if cuts else 1.0
    drawn = jax.random.normal(rng, shape, jnp.float32) * spread * level
    return jnp.minimum(jnp.maximum(drawn, -limit), limit).astype(kind)


def heavy_noise(rng, dims, width, most, pieces, heavy, held_as=jnp.bfloat16):
    values = width * jax.random.normal(rng, dims, jnp.float32)
    if pieces:
        values = values * block_levels(rng, dims, pieces, -0.22, 0.18)
    return jnp.clip(raised(values, jax.random.fold_in(rng, 3), *heavy), -most, most).astype(held_as)


def setup_inputs(seed: int = 0) -> dict:
    key_of = jax.random.split(jax.random.key(seed), 12)
    return {
        "query_branch": heavy_noise(key_of[0], (SEQS, SEQLEN, OPERATOR_WIDTH), 1.0, 6.0, ((0, 4), (1, 32)), (1, 2, 32, 2.75)),
        "key_branch": normal_values(key_of[1], (SEQS, SEQLEN, OPERATOR_WIDTH), 1.0, 6.0, ((0, 4), (1, 32))),
        "value_branch": normal_values(key_of[2], (SEQS, SEQLEN, OPERATOR_WIDTH), 1.0, 6.0, ((0, 4), (1, 32))),
        "cotangent": normal_values(key_of[3], (SEQS, SEQLEN, OUTPUT_FEATURES), 1.0, 6.0, ((0, 4), (1, 32))),
        "quantized_weight_codes": touch_ends(jax.random.randint(key_of[4], (OPERATOR_WIDTH, OUTPUT_FEATURES), 0, 16), jax.random.fold_in(key_of[4], 1), 0, 15).astype(jnp.int32),
        "scale_code_bytes": touch_ends(jax.random.randint(key_of[5], (OPERATOR_WIDTH, SCALE_COLS), 0, 256), jax.random.fold_in(key_of[5], 1), 0, 255).astype(jnp.int32),
        "row_scale_second": jnp.clip(jnp.exp(math.log(0.1) - 2.3025851 * jax.random.uniform(key_of[6], (OPERATOR_WIDTH,), jnp.float32) ** block_levels(key_of[6], (OPERATOR_WIDTH,), ((0, 32),), -0.2, 0.2)), 0.01, 0.1),
        "filters": normal_values(key_of[7], (GROUPS, FL), FL ** -0.5, 0.5),
        "channel_skip_weight": normal_values(key_of[8], (OPERATOR_WIDTH,), 1.0, 6.0, (), jnp.float32),
        "adapter_down_weight": normal_values(key_of[9], (OPERATOR_WIDTH, ADAPTER_RANK), OPERATOR_WIDTH ** -0.5, 0.09375, ((0, 32),)),
        "adapter_up_weight": normal_values(key_of[10], (ADAPTER_RANK, OUTPUT_FEATURES), ADAPTER_RANK ** -0.5, 0.75, ((1, 4),)),
    }


normal_levels = (-1.0, -0.6961928009986877, -0.5250730514526367, -0.39491748809814453, -0.28444138169288635, -0.18477343022823334, -0.09105003625154495, 0.0, 0.07958029955625534, 0.16093020141124725, 0.24611230194568634, 0.33791524171829224, 0.44070982933044434, 0.5626170039176941, 0.7229568362236023, 1.0)
adapter_scale = 0.25

def dequantize(quantized_weight_codes, scale_code_bytes, row_scale_second):
    level_table = jnp.array(normal_levels, jnp.float32)
    levels = level_table[quantized_weight_codes]
    absmax = row_scale_second[:, None] * (scale_code_bytes.astype(jnp.float32) + 1.0) / 256.0
    absmax = jnp.repeat(absmax, QBLOCK, axis=1)
    return (levels * absmax).astype(jnp.bfloat16)

def toeplitz(filter_taps, filter_len):
    groups = filter_taps.shape[0]
    padded = jnp.concatenate([filter_taps, jnp.zeros((groups, filter_len), filter_taps.dtype)], 1)
    repeated = jnp.tile(padded, (1, filter_len))[:, :filter_len * (2 * filter_len - 1)]
    return repeated.reshape(groups, filter_len, 2 * filter_len - 1)

def block_conv(extended, toep, filter_len):
    row_count = extended.shape[0] - (filter_len - 1)
    blocks = row_count // filter_len
    current = extended[:row_count].reshape(blocks, filter_len, -1)
    following = jnp.concatenate([extended[filter_len:], jnp.zeros((1, extended.shape[1]), extended.dtype)], 0)
    following = following.reshape(blocks, filter_len, -1)[:, :filter_len - 1]
    windows = jnp.concatenate([current, following], 1)
    windows = windows.reshape(blocks, 2 * filter_len - 1, toep.shape[0], -1)
    result = jnp.einsum('gts,bsgk->btgk', toep.astype(jnp.float32), windows.astype(jnp.float32))
    return result.reshape(row_count, -1)

def reference(query_branch, key_branch, value_branch, cotangent, quantized_weight_codes, scale_code_bytes, row_scale_second, filters, channel_skip_weight, adapter_down_weight, adapter_up_weight):
    filter_len = filters.shape[1]
    channels = query_branch.shape[2]
    weight_matrix = dequantize(quantized_weight_codes, scale_code_bytes, row_scale_second)
    ahead_toep = toeplitz(jnp.flip(filters, 1), filter_len)
    back_toep = toeplitz(filters, filter_len)
    multiplier = adapter_scale / math.sqrt(query_branch.shape[0] * query_branch.shape[1])
    outputs, grad_queries, grad_keys, grad_values = ([], [], [], [])
    down_accumulator = jnp.zeros(adapter_down_weight.shape, jnp.float32)
    up_accumulator = jnp.zeros(adapter_up_weight.shape, jnp.float32)
    for sequence in range(query_branch.shape[0]):
        query_float = query_branch[sequence].astype(jnp.float32)
        key_float = key_branch[sequence].astype(jnp.float32)
        value_float = value_branch[sequence].astype(jnp.float32)
        output_gradient = cotangent[sequence]
        mixed = (key_float * value_float).astype(jnp.bfloat16)
        extended = jnp.concatenate([jnp.zeros((filter_len - 1, channels), mixed.dtype), mixed], 0)
        gated = block_conv(extended, ahead_toep, filter_len) + channel_skip_weight * mixed.astype(jnp.float32)
        gated_signal = (query_float * gated).astype(jnp.bfloat16)
        down_projection = jnp.dot(gated_signal, adapter_down_weight, preferred_element_type=jnp.float32).astype(jnp.bfloat16)
        output = jnp.dot(gated_signal, weight_matrix, preferred_element_type=jnp.float32) + adapter_scale * jnp.dot(down_projection, adapter_up_weight, preferred_element_type=jnp.float32)
        outputs.append(output.astype(jnp.bfloat16))
        backward_up_term = jnp.dot(output_gradient, adapter_up_weight.T, preferred_element_type=jnp.float32).astype(jnp.bfloat16)
        backward_gradient = jnp.dot(output_gradient, weight_matrix.T, preferred_element_type=jnp.float32) + adapter_scale * jnp.dot(backward_up_term, adapter_down_weight.T, preferred_element_type=jnp.float32)
        grad_queries.append((backward_gradient * gated).astype(jnp.bfloat16))
        grad_gated = (backward_gradient * query_float).astype(jnp.bfloat16)
        extended_back = jnp.concatenate([grad_gated, jnp.zeros((filter_len - 1, channels), grad_gated.dtype)], 0)
        grad_mixed = block_conv(extended_back, back_toep, filter_len) + channel_skip_weight * grad_gated.astype(jnp.float32)
        grad_keys.append((grad_mixed * value_float).astype(jnp.bfloat16))
        grad_values.append((grad_mixed * key_float).astype(jnp.bfloat16))
        down_accumulator = down_accumulator + jnp.dot(gated_signal.T, backward_up_term, preferred_element_type=jnp.float32)
        up_accumulator = up_accumulator + jnp.dot(down_projection.T, output_gradient, preferred_element_type=jnp.float32)
    return (jnp.stack(outputs), jnp.stack(grad_queries), jnp.stack(grad_keys), jnp.stack(grad_values), (multiplier * down_accumulator).astype(jnp.bfloat16), (multiplier * up_accumulator).astype(jnp.bfloat16))
```

```python
import functools
import math

import jax
import jax.numpy as jnp
from jax import lax
from jax.experimental import pallas as pl
from jax.experimental.pallas import tpu as pltpu
from jax.sharding import PartitionSpec as P

QBLOCK = 64
BOTH = ("fsdp", "ctx")
RING = (0, 3, 1, 2)

normal_levels = (
    -1.0,
    -0.6961928009986877,
    -0.5250730514526367,
    -0.39491748809814453,
    -0.28444138169288635,
    -0.18477343022823334,
    -0.09105003625154495,
    0.0,
    0.07958029955625534,
    0.16093020141124725,
    0.24611230194568634,
    0.33791524171829224,
    0.44070982933044434,
    0.5626170039176941,
    0.7229568362236023,
    1.0,
)
adapter_scale = 0.25


def device_index(x, y, z, c):
    return ((x // 2) * 2 + c) * 32 + y * 8 + z * 2 + x % 2


def ring_pairs(axis0, axis1, step):
    pairs = []
    for x in range(4):
        for y in range(4):
            for z in range(4):
                for c in range(2):
                    to = [x, y, z]
                    axis = (axis0, axis1)[c]
                    to[axis] = (to[axis] + step) % 4
                    pairs.append((device_index(x, y, z, c), device_index(*to, c)))
    return pairs


def send(block, axis0, axis1, step):
    return lax.ppermute(block, BOTH, ring_pairs(axis0, axis1, step))


def swap_cores(block):
    pairs = [
        (device_index(x, y, z, c), device_index(x, y, z, 1 - c))
        for x in range(4)
        for y in range(4)
        for z in range(4)
        for c in range(2)
    ]
    return lax.ppermute(block, BOTH, pairs)


def ring_phase(block, axis0, axis1):
    half = block.shape[0] // 2
    plus = send(block, axis0, axis1, 1)
    minus = send(block, axis0, axis1, -1)
    far_low = send(plus[:half], axis0, axis1, 1)
    far_high = send(minus[half:], axis0, axis1, -1)
    return plus, minus, far_low, far_high


def along_ctx(shard, by):
    pairs = [(i, i + by) for i in range(32) if 0 <= i + by < 32]
    return lax.ppermute(shard, "ctx", pairs)


def weight_piece(codes, scale_bytes, row_scale, down, up):
    levels = jnp.zeros(codes.shape, jnp.float32)
    for number in range(16):
        levels = jnp.where(codes == number, normal_levels[number], levels)
    absmax = row_scale[:, None] * (scale_bytes.astype(jnp.float32) + 1.0) / 256.0
    absmax = jnp.repeat(absmax, QBLOCK, axis=1)
    weight = (levels * absmax).astype(jnp.bfloat16).astype(jnp.float32)
    low_rank = jnp.dot(down, up, preferred_element_type=jnp.float32)
    return (weight + adapter_scale * low_rank).astype(jnp.bfloat16)


def toeplitz_conv(base, window, width):
    lane = lax.broadcasted_iota(jnp.int32, (128, 2 * width), 1)
    group_of = (lane % width) // 16
    total = None
    for group in range(width // 16):
        row = jnp.broadcast_to(base[group : group + 1, :], (128, 256))
        toep = pltpu.roll(row, 0, 1, stride=1, stride_axis=0).astype(jnp.bfloat16)
        part = jnp.dot(toep, window, preferred_element_type=jnp.float32)
        total = part if total is None else jnp.where(group_of == group, part, total)
    return total


def forward_kernel(base_ref, skip_ref, query_ref, key_ref, value_ref, halo_ref, gated_ref, signal_ref, *, tiles):
    for tile in range(tiles):
        lanes = pl.ds(tile * 128, 128)
        mixed = (
            key_ref[:, lanes].astype(jnp.float32) * value_ref[:, lanes].astype(jnp.float32)
        ).astype(jnp.bfloat16)
        first = jnp.concatenate([halo_ref[:, lanes], mixed[:128]], 0)
        window = jnp.concatenate([first, mixed], 1)
        conv = toeplitz_conv(base_ref[pl.ds(tile * 8, 8), :], window, 128)
        conv = jnp.concatenate([conv[:, :128], conv[:, 128:]], 0)
        gated = conv + skip_ref[:, lanes] * mixed.astype(jnp.float32)
        gated_ref[:, lanes] = gated
        signal_ref[:, lanes] = (query_ref[:, lanes].astype(jnp.float32) * gated).astype(jnp.bfloat16)


def forward_conv(base, skip, query, key, value, halo):
    rows, channels = query.shape
    width = 512
    block = pl.BlockSpec((rows, width), lambda j: (0, j))
    return pl.pallas_call(
        functools.partial(forward_kernel, tiles=width // 128),
        grid=(channels // width,),
        in_specs=[
            pl.BlockSpec((width // 16, 256), lambda j: (j, 0)),
            pl.BlockSpec((1, width), lambda j: (0, j)),
            block,
            block,
            block,
            pl.BlockSpec((128, width), lambda j: (0, j)),
        ],
        out_specs=[block, block],
        out_shape=[
            jax.ShapeDtypeStruct((rows, channels), jnp.float32),
            jax.ShapeDtypeStruct((rows, channels), jnp.bfloat16),
        ],
        compiler_params=pltpu.CompilerParams(vmem_limit_bytes=32 << 20),
        cost_estimate=pl.CostEstimate(flops=1 << 32, bytes_accessed=14 << 20, transcendentals=0),
        name="forward_conv",
    )(base, skip, query, key, value, halo)


def backward_kernel(
    base_ref, skip_ref, back_ref, gated_ref, query_ref, query_halo_ref, key_ref, value_ref,
    grad_query_ref, grad_key_ref, grad_value_ref, *, tiles,
):
    rows = query_ref.shape[0]
    for tile in range(tiles):
        lanes = pl.ds(tile * 128, 128)
        back = back_ref[pl.ds(0, rows), lanes]
        grad_query_ref[:, lanes] = (back * gated_ref[:, lanes]).astype(jnp.bfloat16)
        here = (back * query_ref[:, lanes].astype(jnp.float32)).astype(jnp.bfloat16)
        ahead = back_ref[pl.ds(rows, 128), lanes] * query_halo_ref[:, lanes].astype(jnp.float32)
        second = jnp.concatenate([here[128:], ahead.astype(jnp.bfloat16)], 0)
        window = jnp.concatenate([here, second], 1)
        conv = toeplitz_conv(base_ref[pl.ds(tile * 8, 8), :], window, 128)
        conv = jnp.concatenate([conv[:, :128], conv[:, 128:]], 0)
        mixed = conv + skip_ref[:, lanes] * here.astype(jnp.float32)
        grad_key_ref[:, lanes] = (mixed * value_ref[:, lanes].astype(jnp.float32)).astype(jnp.bfloat16)
        grad_value_ref[:, lanes] = (mixed * key_ref[:, lanes].astype(jnp.float32)).astype(jnp.bfloat16)


def backward_conv(base, skip, back, gated, query, query_halo, key, value):
    rows, channels = query.shape
    width = 512
    block = pl.BlockSpec((rows, width), lambda j: (0, j))
    result = jax.ShapeDtypeStruct((rows, channels), jnp.bfloat16)
    return pl.pallas_call(
        functools.partial(backward_kernel, tiles=width // 128),
        grid=(channels // width,),
        in_specs=[
            pl.BlockSpec((width // 16, 256), lambda j: (j, 0)),
            pl.BlockSpec((1, width), lambda j: (0, j)),
            pl.BlockSpec((rows + 128, width), lambda j: (0, j)),
            block,
            block,
            pl.BlockSpec((128, width), lambda j: (0, j)),
            block,
            block,
        ],
        out_specs=[block] * 3,
        out_shape=[result] * 3,
        compiler_params=pltpu.CompilerParams(vmem_limit_bytes=32 << 20),
        cost_estimate=pl.CostEstimate(flops=1 << 32, bytes_accessed=24 << 20, transcendentals=0),
        name="backward_conv",
    )(base, skip, back, gated, query, query_halo, key, value)


def project_kernel(*refs, groups, first, last):
    refs = list(refs)
    meta = refs.pop(0)
    signal_ref, cot_ref = refs.pop(0), refs.pop(0)
    if not first:
        out_in, back_in = refs.pop(0), refs.pop(0)
    arrays = [[refs.pop(0) for _ in range(count)] for _, _, count in groups]
    out_ref, back_ref = refs.pop(0), refs.pop(0)
    signal, cot, out_acc, back_acc, held, sems, io_sems = refs
    x0, y0, z0, core = meta[0], meta[1], meta[2], meta[3]
    loads = [
        pltpu.make_async_copy(signal_ref, signal, io_sems.at[0]),
        pltpu.make_async_copy(cot_ref, cot, io_sems.at[1]),
    ]
    if not first:
        loads.append(pltpu.make_async_copy(out_in, out_acc, io_sems.at[2]))
        loads.append(pltpu.make_async_copy(back_in, back_acc, io_sems.at[3]))
    for load in loads:
        load.start()
    copies = []
    for g, (mine, _, count) in enumerate(groups):
        chain = core if mine else 1 - core
        group = []
        for n in range(16):
            a, b = RING[n // 4], RING[n % 4]
            x = (x0 + jnp.where(chain == 0, b, a)) & 3
            w = jnp.where(chain == 0, y0 + a, z0 + b) & 3
            slot = pl.multiple_of((w * 4 + x) * 128, 128)
            each = 16 // count
            source = arrays[g][n // each].at[pl.ds((n % each) * 128, 128), :]
            group.append(
                pltpu.make_async_copy(source, held.at[g, pl.ds(slot, 128), :], sems.at[g, n])
            )
        for copy in group:
            copy.start()
        copies.append(group)
    if first:
        out_acc[...] = jnp.zeros_like(out_acc)
        back_acc[...] = jnp.zeros_like(back_acc)
    for load in loads:
        load.wait()
    for g, (mine, offset, _) in enumerate(groups):
        chain = core if mine else 1 - core
        fixed = jnp.where(chain == 0, z0 + offset, y0 + offset) & 3
        for copy in copies[g]:
            copy.wait()

        @pl.loop(0, 8)
        def _(step, g=g, chain=chain, fixed=fixed):
            w, xh = step // 2, step % 2
            rows = jnp.where(chain == 0, w * 4 + fixed, fixed * 4 + w)
            rows = pl.multiple_of(rows * 256, 256)
            cols = pl.multiple_of((xh * 2 + chain) * 1024, 1024)
            weight = held[g, pl.ds(pl.multiple_of(step * 256, 256), 256), :]
            out_acc[:, pl.ds(cols, 1024)] += jnp.dot(
                signal[:, pl.ds(rows, 256)], weight, preferred_element_type=jnp.float32
            )
            back_acc[:, pl.ds(rows, 256)] += lax.dot_general(
                cot[:, pl.ds(cols, 1024)],
                weight,
                (((1,), (1,)), ((), ())),
                preferred_element_type=jnp.float32,
            )

    if last:
        signal[...] = out_acc[...].astype(jnp.bfloat16)
        stores = [pltpu.make_async_copy(signal, out_ref, io_sems.at[0])]
    else:
        stores = [pltpu.make_async_copy(out_acc, out_ref, io_sems.at[0])]
    stores.append(pltpu.make_async_copy(back_acc, back_ref, io_sems.at[1]))
    for store in stores:
        store.start()
    for store in stores:
        store.wait()


def project(meta, signal, cot, sums, groups, last):
    rows, channels = signal.shape
    first = sums is None
    arrays = [array for group in groups for array in group[2]]
    static = tuple((mine, offset, len(held)) for mine, offset, held in groups)
    anywhere = pl.BlockSpec(memory_space=pl.ANY)
    out_type = jnp.bfloat16 if last else jnp.float32
    operands = [meta, signal, cot] + ([] if first else list(sums)) + arrays
    aliases = {} if first else ({4: 1} if last else {3: 0, 4: 1})
    flops = len(groups) * 16 * 128 * 1024 * (rows + cot.shape[0]) * 2
    return pl.pallas_call(
        functools.partial(project_kernel, groups=static, first=first, last=last),
        in_specs=[pl.BlockSpec(memory_space=pltpu.SMEM)] + [anywhere] * (len(operands) - 1),
        out_specs=[anywhere, anywhere],
        out_shape=[
            jax.ShapeDtypeStruct((rows, channels), out_type),
            jax.ShapeDtypeStruct((cot.shape[0], channels), jnp.float32),
        ],
        scratch_shapes=[
            pltpu.VMEM((rows, channels), jnp.bfloat16),
            pltpu.VMEM((cot.shape[0], channels), jnp.bfloat16),
            pltpu.VMEM((rows, channels), jnp.float32),
            pltpu.VMEM((cot.shape[0], channels), jnp.float32),
            pltpu.VMEM((len(groups), 2048, 1024), jnp.bfloat16),
            pltpu.SemaphoreType.DMA((len(groups), 16)),
            pltpu.SemaphoreType.DMA((4,)),
        ],
        input_output_aliases=aliases,
        compiler_params=pltpu.CompilerParams(vmem_limit_bytes=48 << 20),
        cost_estimate=pl.CostEstimate(
            flops=flops, bytes_accessed=len(groups) * (4 << 20) + (25 << 20), transcendentals=0
        ),
        name="project",
    )(*operands)


def adapter_gradients(signal, cot, down_piece, up_piece, multiplier):
    rank = up_piece.shape[0]
    up = lax.all_gather(up_piece, "fsdp", axis=1, tiled=True)
    spread = jnp.broadcast_to(down_piece.T[None], (32, rank, 128))
    down = lax.all_to_all(spread, "ctx", 0, 0, tiled=True)
    down = jnp.transpose(down, (1, 0, 2)).reshape(rank, 4096)
    down_projection = lax.dot_general(
        signal, down, (((1,), (1,)), ((), ())), preferred_element_type=jnp.float32
    ).astype(jnp.bfloat16)
    back_up = lax.dot_general(
        cot, up, (((1,), (1,)), ((), ())), preferred_element_type=jnp.float32
    ).astype(jnp.bfloat16)
    over_rows = (((0,), (0,)), ((), ()))
    term_down = lax.dot_general(back_up, signal, over_rows, preferred_element_type=jnp.float32)
    term_up = lax.dot_general(down_projection, cot, over_rows, preferred_element_type=jnp.float32)
    parts_down = term_down.astype(jnp.bfloat16).reshape(4, 16, 32, 128)
    parts_down = jnp.transpose(parts_down, (0, 2, 1, 3)).reshape(128, 16, 128)
    parts_up = term_up.astype(jnp.bfloat16).reshape(32, 2, 4, 1024)
    parts_up = jnp.transpose(parts_up, (2, 0, 1, 3)).reshape(128, 16, 128)
    parts = jnp.concatenate([parts_down, parts_up], 1)
    parts = lax.all_to_all(parts, BOTH, 0, 0, tiled=True)
    sums = (multiplier * jnp.sum(parts.astype(jnp.float32), 0)).astype(jnp.bfloat16)
    grad_down = lax.all_gather(sums[:16], "fsdp", axis=0, tiled=True)
    mine_up = jnp.broadcast_to(sums[None, 16:], (32, 16, 128))
    grad_up = lax.all_to_all(mine_up, "ctx", 0, 0, tiled=True).reshape(rank, 1024)
    return grad_down.T, grad_up


def local(
    query_branch,
    key_branch,
    value_branch,
    cotangent,
    quantized_weight_codes,
    scale_code_bytes,
    row_scale_second,
    filters,
    channel_skip_weight,
    adapter_down_weight,
    adapter_up_weight,
):
    query, key, value, cot = query_branch[0], key_branch[0], value_branch[0], cotangent[0]
    rows, channels = query.shape
    multiplier = adapter_scale / math.sqrt(4 * 8192)
    ctx, fsdp = lax.axis_index("ctx"), lax.axis_index("fsdp")
    core = fsdp % 2
    meta = jnp.stack([(fsdp // 2) * 2 + ctx % 2, ctx // 8, (ctx // 2) % 4, core]).astype(jnp.int32)

    piece = weight_piece(
        quantized_weight_codes, scale_code_bytes, row_scale_second, adapter_down_weight, adapter_up_weight
    )
    plus, minus, low, high = ring_phase(piece, 0, 2)
    held = jnp.concatenate([piece, plus, minus, low, high], 0)
    plus, minus, low, high = ring_phase(held, 1, 0)
    held = jnp.concatenate([held, plus, minus, low, high], 0)
    plus, minus, low, high = ring_phase(held, 2, 1)

    mixed_tail = (key[128:].astype(jnp.float32) * value[128:].astype(jnp.float32)).astype(jnp.bfloat16)
    mixed_halo = along_ctx(mixed_tail, 1)
    query_halo = along_ctx(query[:128], -1)
    cot_halo = along_ctx(cot[:128], -1)

    taps = filters.astype(jnp.float32)
    forward_base = jnp.pad(jnp.flip(taps, 1), ((0, 0), (1, 127)))
    backward_base = jnp.pad(taps, ((0, 0), (0, 128)))
    skip = channel_skip_weight[None]
    gated, signal = forward_conv(forward_base, skip, query, key, value, mixed_halo)

    grad_down, grad_up = adapter_gradients(signal, cot, adapter_down_weight, adapter_up_weight, multiplier)

    cot_rows = jnp.concatenate([cot, cot_halo], 0)
    sums = project(
        meta, signal, cot_rows, None, [(True, 0, [held]), (False, 0, [swap_cores(held)])], False
    )
    sums = project(
        meta,
        signal,
        cot_rows,
        sums,
        [
            (True, -1, [plus]),
            (False, -1, [swap_cores(plus)]),
            (True, 1, [minus]),
            (False, 1, [swap_cores(minus)]),
        ],
        False,
    )
    output, back = project(
        meta,
        signal,
        cot_rows,
        sums,
        [(True, 2, [low, high]), (False, 2, [swap_cores(low), swap_cores(high)])],
        True,
    )
    grad_query, grad_key, grad_value = backward_conv(
        backward_base, skip, back, gated, query, query_halo, key, value
    )
    return output[None], grad_query[None], grad_key[None], grad_value[None], grad_down, grad_up


def solution(mesh):
    return jax.shard_map(
        local,
        mesh=mesh,
        in_specs=(
            P("fsdp", "ctx", None),
            P("fsdp", "ctx", None),
            P("fsdp", "ctx", None),
            P("fsdp", "ctx", None),
            P("ctx", "fsdp"),
            P("ctx", "fsdp"),
            P("ctx"),
            P(),
            P(),
            P("ctx", None),
            P(None, "fsdp"),
        ),
        out_specs=(
            P("fsdp", "ctx", None),
            P("fsdp", "ctx", None),
            P("fsdp", "ctx", None),
            P("fsdp", "ctx", None),
            P("ctx", None),
            P(None, "fsdp"),
        ),
        check_vma=False,
    )
```

```python
import functools
import math

import jax
import jax.numpy as jnp
from jax import lax
from jax.experimental import pallas as pl
from jax.experimental.pallas import tpu as pltpu
from jax.sharding import PartitionSpec as P

QBLOCK = 64
BOTH = ("fsdp", "ctx")
RING = (0, 3, 1, 2)

normal_levels = (
    -1.0,
    -0.6961928009986877,
    -0.5250730514526367,
    -0.39491748809814453,
    -0.28444138169288635,
    -0.18477343022823334,
    -0.09105003625154495,
    0.0,
    0.07958029955625534,
    0.16093020141124725,
    0.24611230194568634,
    0.33791524171829224,
    0.44070982933044434,
    0.5626170039176941,
    0.7229568362236023,
    1.0,
)
adapter_scale = 0.25


def device_index(x, y, z, c):
    return ((x // 2) * 2 + c) * 32 + y * 8 + z * 2 + x % 2


def ring_pairs(axis0, axis1, step):
    pairs = []
    for x in range(4):
        for y in range(4):
            for z in range(4):
                for c in range(2):
                    to = [x, y, z]
                    axis = (axis0, axis1)[c]
                    to[axis] = (to[axis] + step) % 4
                    pairs.append((device_index(x, y, z, c), device_index(*to, c)))
    return pairs


def send(block, axis0, axis1, step):
    return lax.ppermute(block, BOTH, ring_pairs(axis0, axis1, step))


def swap_cores(block):
    pairs = [
        (device_index(x, y, z, c), device_index(x, y, z, 1 - c))
        for x in range(4)
        for y in range(4)
        for z in range(4)
        for c in range(2)
    ]
    return lax.ppermute(block, BOTH, pairs)


def ring_phase(block, axis0, axis1):
    half = block.shape[0] // 2
    plus = send(block, axis0, axis1, 1)
    minus = send(block, axis0, axis1, -1)
    far_low = send(plus[:half], axis0, axis1, 1)
    far_high = send(minus[half:], axis0, axis1, -1)
    return plus, minus, far_low, far_high


def after(block, *earlier):
    return lax.optimization_barrier((block, earlier))[0]


def along_ctx(shard, by):
    pairs = [(i, i + by) for i in range(32) if 0 <= i + by < 32]
    return lax.ppermute(shard, "ctx", pairs)


def next_rows(block, ctx):
    xl, z = ctx % 2, (ctx // 2) % 4
    along_y = [(i, i + 8) for i in range(32) if i % 8 == 7 and i + 8 < 32]
    relayed = lax.ppermute(block, "ctx", along_y)
    along_z = [
        (i, i + 2 if i % 8 != 7 else i - 6) for i in range(32) if i % 2 == 1 and (i % 8 != 7 or i >= 15)
    ]
    block_z = jnp.where(z == 3, relayed, block)
    relayed = lax.ppermute(block_z, "ctx", along_z)
    return relayed


def pair_rows(block, relayed, ctx):
    crossed = lax.ppermute(
        jnp.where(ctx % 2 == 0, block, relayed), "ctx", [(i, i ^ 1) for i in range(32)]
    )
    return jnp.where(ctx == 0, jnp.zeros_like(crossed), crossed)


def weight_piece(codes, scale_bytes, row_scale, down, up):
    levels = jnp.zeros(codes.shape, jnp.float32)
    for number in range(16):
        levels = jnp.where(codes == number, normal_levels[number], levels)
    absmax = row_scale[:, None] * (scale_bytes.astype(jnp.float32) + 1.0) / 256.0
    absmax = jnp.repeat(absmax, QBLOCK, axis=1)
    weight = (levels * absmax).astype(jnp.bfloat16).astype(jnp.float32)
    low_rank = jnp.dot(down, up, preferred_element_type=jnp.float32)
    return (weight + adapter_scale * low_rank).astype(jnp.bfloat16)


def toeplitz_conv(base, window, width):
    lane = lax.broadcasted_iota(jnp.int32, (128, 2 * width), 1)
    group_of = (lane % width) // 16
    total = None
    for group in range(width // 16):
        row = jnp.broadcast_to(base[group : group + 1, :], (128, 256))
        toep = pltpu.roll(row, 0, 1, stride=1, stride_axis=0).astype(jnp.bfloat16)
        part = jnp.dot(toep, window, preferred_element_type=jnp.float32)
        total = part if total is None else jnp.where(group_of == group, part, total)
    return total


def forward_kernel(base_ref, skip_ref, query_ref, key_ref, value_ref, halo_ref, gated_ref, signal_ref, *, tiles):
    for tile in range(tiles):
        lanes = pl.ds(tile * 128, 128)
        mixed = (
            key_ref[:, lanes].astype(jnp.float32) * value_ref[:, lanes].astype(jnp.float32)
        ).astype(jnp.bfloat16)
        first = jnp.concatenate([halo_ref[:, lanes], mixed[:128]], 0)
        window = jnp.concatenate([first, mixed], 1)
        conv = toeplitz_conv(base_ref[pl.ds(tile * 8, 8), :], window, 128)
        conv = jnp.concatenate([conv[:, :128], conv[:, 128:]], 0)
        gated = conv + skip_ref[:, lanes] * mixed.astype(jnp.float32)
        gated_ref[:, lanes] = gated
        signal_ref[:, lanes] = (query_ref[:, lanes].astype(jnp.float32) * gated).astype(jnp.bfloat16)


def forward_conv(base, skip, query, key, value, halo):
    rows, channels = query.shape
    width = 512
    block = pl.BlockSpec((rows, width), lambda j: (0, j))
    return pl.pallas_call(
        functools.partial(forward_kernel, tiles=width // 128),
        grid=(channels // width,),
        in_specs=[
            pl.BlockSpec((width // 16, 256), lambda j: (j, 0)),
            pl.BlockSpec((1, width), lambda j: (0, j)),
            block,
            block,
            block,
            pl.BlockSpec((128, width), lambda j: (0, j)),
        ],
        out_specs=[block, block],
        out_shape=[
            jax.ShapeDtypeStruct((rows, channels), jnp.float32),
            jax.ShapeDtypeStruct((rows, channels), jnp.bfloat16),
        ],
        compiler_params=pltpu.CompilerParams(vmem_limit_bytes=54 << 20),
        cost_estimate=pl.CostEstimate(flops=1 << 32, bytes_accessed=14 << 20, transcendentals=0),
        name="forward_conv",
    )(base, skip, query, key, value, halo)


def backward_kernel(
    base_ref, skip_ref, head_ref, tail_ref, halo_ref, key_ref, value_ref, *refs, tiles
):
    grad_key_ref, grad_value_ref = refs[-2:]
    for tile in range(tiles):
        lanes = pl.ds(tile * 128, 128)
        here = jnp.concatenate([head_ref[:, lanes], tail_ref[:, lanes]], 0)
        second = jnp.concatenate([tail_ref[:, lanes], halo_ref[:, lanes]], 0)
        window = jnp.concatenate([here, second], 1)
        conv = toeplitz_conv(base_ref[pl.ds(tile * 8, 8), :], window, 128)
        conv = jnp.concatenate([conv[:, :128], conv[:, 128:]], 0)
        mixed = conv + skip_ref[:, lanes] * here.astype(jnp.float32)
        grad_key_ref[:, lanes] = (mixed * value_ref[:, lanes].astype(jnp.float32)).astype(jnp.bfloat16)
        grad_value_ref[:, lanes] = (mixed * key_ref[:, lanes].astype(jnp.float32)).astype(jnp.bfloat16)


def backward_conv(base, skip, head, tail, halo, key, value, part, results):
    rows, channels = key.shape
    width = 512
    skipped = part * (channels // 2 // width)
    block = pl.BlockSpec((rows, width), lambda j: (0, j + skipped))
    half = pl.BlockSpec((128, width), lambda j: (0, j))
    anywhere = pl.BlockSpec(memory_space=pl.ANY)
    return pl.pallas_call(
        functools.partial(backward_kernel, tiles=width // 128),
        grid=(channels // 2 // width,),
        in_specs=[
            pl.BlockSpec((width // 16, 256), lambda j: (j + skipped, 0)),
            pl.BlockSpec((1, width), lambda j: (0, j + skipped)),
            half,
            pl.BlockSpec((128, width), lambda j: (0, j + skipped)),
            half,
            block,
            block,
        ]
        + [anywhere] * len(results),
        out_specs=[block] * 2,
        out_shape=[jax.ShapeDtypeStruct((rows, channels), jnp.bfloat16)] * 2,
        input_output_aliases={7: 0, 8: 1} if results else {},
        compiler_params=pltpu.CompilerParams(vmem_limit_bytes=54 << 20),
        cost_estimate=pl.CostEstimate(flops=1 << 31, bytes_accessed=6 << 20, transcendentals=0),
        name="backward_conv",
    )(base, skip, head, tail, halo, key, value, *results)


def project_kernel(*refs, groups, first, last):
    refs = list(refs)
    meta = refs.pop(0)
    signal_ref, cot_ref = refs.pop(0), refs.pop(0)
    if not first:
        out_in, back_in = refs.pop(0), refs.pop(0)
    arrays = [[refs.pop(0) for _ in range(count)] for _, _, count in groups]
    if last:
        gated_ref, query_ref, out_ref, grad_query_ref, *head_refs = refs[:6]
        tail_ref, refs = refs[6], refs[7:]
    else:
        out_ref, back_ref = refs[:2]
        refs = refs[2:]
    signal, picked, cot, out_acc, back_acc, held, sems, io_sems = refs[:8]
    x0, y0, z0, core = meta[0], meta[1], meta[2], meta[3]
    rows = signal.shape[0]
    loads = [
        pltpu.make_async_copy(signal_ref, signal, io_sems.at[0]),
        pltpu.make_async_copy(cot_ref, cot, io_sems.at[1]),
    ]
    if not first:
        loads.append(pltpu.make_async_copy(out_in, out_acc, io_sems.at[3]))
        loads.append(pltpu.make_async_copy(back_in, back_acc, io_sems.at[4]))
    for load in loads:
        load.start()
    copies = []
    for g, (mine, _, count) in enumerate(groups):
        chain = core if mine else 1 - core
        each = 16 // count
        group = []
        for n in range(16):
            a, b = RING[n // 4], RING[n % 4]
            x = (x0 + jnp.where(chain == 0, b, a)) & 3
            w = jnp.where(chain == 0, y0 + a, z0 + b) & 3
            slot = pl.multiple_of(((x >> 1) * 8 + w * 2 + (x & 1)) * 128, 128)
            source = arrays[g][n // each].at[pl.ds((n % each) * 128, 128), :]
            group.append(
                pltpu.make_async_copy(source, held.at[g, pl.ds(slot, 128), :], sems.at[g, n])
            )
        copies.append(group)
    for group in copies[:2]:
        for copy in group:
            copy.start()
    late = []
    if last:
        gated, query, gradient = refs[8:11]
        for n, (source, target) in enumerate([(gated_ref, gated), (query_ref, query)]):
            late.append(pltpu.make_async_copy(source, target, io_sems.at[5 + n]))
    if first:
        out_acc[...] = jnp.zeros_like(out_acc)
        back_acc[...] = jnp.zeros_like(back_acc)
    for load in loads:
        load.wait()
    for g, (mine, offset, _) in enumerate(groups):
        chain = core if mine else 1 - core
        fixed = jnp.where(chain == 0, z0 + offset, y0 + offset) & 3

        def channels(w, chain=chain, fixed=fixed):
            return pl.multiple_of(jnp.where(chain == 0, w * 4 + fixed, fixed * 4 + w) * 256, 256)

        for w in range(4):
            picked[:, w * 256 : (w + 1) * 256] = signal[:, pl.ds(channels(w), 256)]
        for copy in copies[g]:
            copy.wait()
        for copy in copies[g + 2] if g + 2 < len(groups) else late if g == 0 else ():
            copy.start()

        @pl.loop(0, 2)
        def _(xh, g=g, chain=chain, channels=channels):
            cols = pl.ds(pl.multiple_of((xh * 2 + chain) * 1024, 1024), 1024)
            weight = held.at[g, pl.ds(pl.multiple_of(xh * 1024, 1024), 1024), :]
            out_acc[:, cols] += jnp.dot(picked[...], weight[...], preferred_element_type=jnp.float32)
            back = lax.dot_general(
                cot[:, cols], weight[...], (((1,), (1,)), ((), ())), preferred_element_type=jnp.float32
            )
            for w in range(4):
                back_acc[:, pl.ds(channels(w), 256)] += back[:, w * 256 : (w + 1) * 256]

    if not last:
        stores = [
            pltpu.make_async_copy(out_acc, out_ref, io_sems.at[0]),
            pltpu.make_async_copy(back_acc, back_ref, io_sems.at[1]),
        ]
        for store in stores:
            store.start()
        for store in stores:
            store.wait()
        return
    signal[...] = out_acc[...].astype(jnp.bfloat16)
    stores = [pltpu.make_async_copy(signal, out_ref, io_sems.at[0])]
    stores[0].start()
    for load in late:
        load.wait()
    for quarter in range(4):

        @pl.loop(0, 4)
        def _(step, quarter=quarter):
            lanes = pl.ds(pl.multiple_of(quarter * 1024 + step * 256, 256), 256)
            back = back_acc[:, lanes]
            gradient[:, lanes] = (back * query[:, lanes].astype(jnp.float32)).astype(jnp.bfloat16)
            query[:, lanes] = (back * gated[:, lanes]).astype(jnp.bfloat16)

        part = pl.ds(quarter * 1024, 1024)
        head = head_refs[quarter // 2].at[:, pl.ds((quarter % 2) * 1024, 1024)]
        for n, (source, target) in enumerate(
            [
                (gradient.at[pl.ds(0, 128), part], head),
                (gradient.at[pl.ds(128, 128), part], tail_ref.at[:, part]),
                (query.at[:, part], grad_query_ref.at[:, part]),
            ]
        ):
            stores.append(pltpu.make_async_copy(source, target, sems.at[0, quarter * 3 + n]))
            stores[-1].start()
    for store in stores:
        store.wait()


def project(meta, signal, cot, sums, groups, finish=None):
    rows, channels = signal.shape
    first, last = sums is None, finish is not None
    arrays = [array for group in groups for array in group[2]]
    static = tuple((mine, offset, len(held)) for mine, offset, held in groups)
    anywhere = pl.BlockSpec(memory_space=pl.ANY)
    operands = [meta, signal, cot] + ([] if first else list(sums)) + arrays
    in_specs = [pl.BlockSpec(memory_space=pltpu.SMEM)] + [anywhere] * (len(operands) - 1)
    flops = len(groups) * 16 * 128 * 1024 * 2 * rows * 2
    moved = len(groups) * (4 << 20) + (16 << 20)
    scratch = [
        pltpu.VMEM((rows, channels), jnp.bfloat16),
        pltpu.VMEM((rows, 1024), jnp.bfloat16),
        pltpu.VMEM((rows, channels), jnp.bfloat16),
        pltpu.VMEM((rows, channels), jnp.float32),
        pltpu.VMEM((rows, channels), jnp.float32),
        pltpu.VMEM((len(groups), 2048, 1024), jnp.bfloat16),
        pltpu.SemaphoreType.DMA((len(groups), 16)),
        pltpu.SemaphoreType.DMA((10,)),
    ]
    if last:
        operands += list(finish)
        in_specs += [anywhere] * 2
        out_shape = [jax.ShapeDtypeStruct((rows, channels), jnp.bfloat16)] * 2
        out_shape += [jax.ShapeDtypeStruct((128, channels // 2), jnp.bfloat16)] * 2
        out_shape += [jax.ShapeDtypeStruct((128, channels), jnp.bfloat16)]
        scratch += [
            pltpu.VMEM((rows, channels), jnp.float32),
            pltpu.VMEM((rows, channels), jnp.bfloat16),
            pltpu.VMEM((rows, channels), jnp.bfloat16),
        ]
        aliases = {}
    else:
        out_shape = [
            jax.ShapeDtypeStruct((rows, channels), jnp.float32),
            jax.ShapeDtypeStruct((rows, channels), jnp.float32),
        ]
        aliases = {} if first else {3: 0, 4: 1}
    return pl.pallas_call(
        functools.partial(project_kernel, groups=static, first=first, last=last),
        in_specs=in_specs,
        out_specs=[anywhere] * len(out_shape),
        out_shape=out_shape,
        scratch_shapes=scratch,
        input_output_aliases=aliases,
        compiler_params=pltpu.CompilerParams(vmem_limit_bytes=54 << 20),
        cost_estimate=pl.CostEstimate(flops=flops, bytes_accessed=moved, transcendentals=0),
        name="project",
    )(*operands)


def gathered_adapters(down_piece, up_piece, ctx, fsdp):
    quarter = lax.dynamic_slice_in_dim(down_piece.T, fsdp * 16, 16, 0)
    block = lax.dynamic_slice(up_piece, ((ctx // 4) * 8, (ctx % 4) * 256), (8, 256))
    block = jnp.concatenate([block[:, :128], block[:, 128:]], 0)
    share = jnp.concatenate([quarter, block], 0)
    shares = lax.all_to_all(jnp.broadcast_to(share[None], (128, 32, 128)), BOTH, 0, 0, tiled=True)
    return shares


def adapter_kernel(signal_ref, cot_ref, shares_ref, parts_ref, down_ref, up_ref):
    for d in range(128):
        fsdp, ctx = d // 32, d % 32
        down_ref[fsdp * 16 : fsdp * 16 + 16, ctx * 128 : ctx * 128 + 128] = shares_ref[d, 0:16, :]
        top, left = (ctx // 4) * 8, fsdp * 1024 + (ctx % 4) * 256
        up_ref[top : top + 8, left : left + 128] = shares_ref[d, 16:24, :]
        up_ref[top : top + 8, left + 128 : left + 256] = shares_ref[d, 24:32, :]
    across = (((1,), (1,)), ((), ()))
    over_rows = (((0,), (0,)), ((), ()))
    down_projection = lax.dot_general(
        signal_ref[...], down_ref[...], across, preferred_element_type=jnp.float32
    ).astype(jnp.bfloat16)
    back_up = lax.dot_general(
        cot_ref[...], up_ref[...], across, preferred_element_type=jnp.float32
    ).astype(jnp.bfloat16)
    down_ref[...] = lax.dot_general(
        back_up, signal_ref[...], over_rows, preferred_element_type=jnp.float32
    ).astype(jnp.bfloat16)
    up_ref[...] = lax.dot_general(
        down_projection, cot_ref[...], over_rows, preferred_element_type=jnp.float32
    ).astype(jnp.bfloat16)
    for d in range(128):
        fsdp, ctx = d // 32, d % 32
        parts_ref[d, 0:16, :] = down_ref[fsdp * 16 : fsdp * 16 + 16, ctx * 128 : ctx * 128 + 128]
        top, left = (ctx // 4) * 8, fsdp * 1024 + (ctx % 4) * 256
        parts_ref[d, 16:24, :] = up_ref[top : top + 8, left : left + 128]
        parts_ref[d, 24:32, :] = up_ref[top : top + 8, left + 128 : left + 256]


def adapter_terms(signal, cot, shares):
    return pl.pallas_call(
        adapter_kernel,
        out_shape=jax.ShapeDtypeStruct((128, 32, 128), jnp.bfloat16),
        scratch_shapes=[pltpu.VMEM((64, 4096), jnp.bfloat16)] * 2,
        compiler_params=pltpu.CompilerParams(vmem_limit_bytes=54 << 20),
        cost_estimate=pl.CostEstimate(flops=1 << 32, bytes_accessed=6 << 20, transcendentals=0),
        name="adapter_terms",
    )(signal, cot, shares)


def adapter_results(parts, multiplier):
    sums = (multiplier * jnp.sum(parts.astype(jnp.float32), 0)).astype(jnp.bfloat16)
    grad_down = lax.all_gather(sums[:16], "fsdp", axis=0, tiled=True)
    up = lax.all_to_all(jnp.broadcast_to(sums[None, 16:], (32, 16, 128)), "ctx", 0, 0, tiled=True)
    grad_up = jnp.transpose(up.reshape(8, 4, 2, 8, 128), (0, 3, 1, 2, 4)).reshape(64, 1024)
    return grad_down.T, grad_up


def local(
    query_branch,
    key_branch,
    value_branch,
    cotangent,
    quantized_weight_codes,
    scale_code_bytes,
    row_scale_second,
    filters,
    channel_skip_weight,
    adapter_down_weight,
    adapter_up_weight,
):
    query, key, value, cot = query_branch[0], key_branch[0], value_branch[0], cotangent[0]
    rows, channels = query.shape
    multiplier = adapter_scale / math.sqrt(4 * 8192)
    ctx, fsdp = lax.axis_index("ctx"), lax.axis_index("fsdp")
    core = fsdp % 2
    meta = jnp.stack([(fsdp // 2) * 2 + ctx % 2, ctx // 8, (ctx // 2) % 4, core]).astype(jnp.int32)

    piece = weight_piece(
        quantized_weight_codes, scale_code_bytes, row_scale_second, adapter_down_weight, adapter_up_weight
    )
    mixed_tail = (key[128:].astype(jnp.float32) * value[128:].astype(jnp.float32)).astype(jnp.bfloat16)
    relayed = next_rows(mixed_tail, ctx)
    plus, minus, low, high = ring_phase(piece, 0, 2)
    held = jnp.concatenate([piece, plus, minus, low, high], 0)
    shares = gathered_adapters(after(adapter_down_weight, held), adapter_up_weight, ctx, fsdp)
    plus, minus, low, high = ring_phase(held, 1, 0)
    front = jnp.concatenate([held, plus], 0)
    rear = after(jnp.concatenate([minus, low, high], 0), front, relayed, shares)
    mixed_halo = pair_rows(mixed_tail, after(relayed, rear), ctx)
    plus_front, minus_front = send(front, 2, 1, 1), send(front, 2, 1, -1)
    plus_rear, minus_rear = send(rear, 2, 1, 1), send(rear, 2, 1, -1)

    taps = filters.astype(jnp.float32)
    forward_base = jnp.pad(jnp.flip(taps, 1), ((0, 0), (1, 127)))
    backward_base = jnp.pad(taps, ((0, 0), (0, 128)))
    skip = channel_skip_weight[None]
    gated, signal = forward_conv(forward_base, skip, query, key, after(value, rear), mixed_halo)

    far_front = send(after(plus_front, signal), 2, 1, 1)
    far_rear = send(minus_rear, 2, 1, -1)
    terms = adapter_terms(signal, cot, shares)
    parts = lax.all_to_all(terms, BOTH, 0, 0, tiled=True)
    swapped = [
        swap_cores(after(block, signal))
        for block in (front, rear, plus_front, plus_rear, minus_front, minus_rear)
    ]
    sums = project(
        meta,
        after(signal, terms),
        cot,
        None,
        [
            (True, 0, [front, rear]),
            (False, 0, swapped[:2]),
            (True, -1, [plus_front, plus_rear]),
            (False, -1, swapped[2:4]),
            (True, 1, [minus_front, minus_rear]),
            (False, 1, swapped[4:]),
        ],
    )
    far = [swap_cores(after(block, sums[0])) for block in (far_front, far_rear)]
    output, grad_query, head_a, head_b, tail = project(
        meta,
        signal,
        cot,
        sums,
        [(True, 2, [far_front, far_rear]), (False, 2, far)],
        (gated, query),
    )
    halo_a, halo_b = along_ctx(head_a, -1), along_ctx(head_b, -1)
    grad_down, grad_up = adapter_results(after(parts, output), multiplier)
    results = backward_conv(backward_base, skip, head_a, tail, halo_a, key, value, 0, ())
    grad_key, grad_value = backward_conv(
        backward_base, skip, head_b, tail, halo_b, key, value, 1, tuple(results)
    )
    return output[None], grad_query[None], grad_key[None], grad_value[None], grad_down, grad_up


def solution(mesh):
    return jax.shard_map(
        local,
        mesh=mesh,
        in_specs=(
            P("fsdp", "ctx", None),
            P("fsdp", "ctx", None),
            P("fsdp", "ctx", None),
            P("fsdp", "ctx", None),
            P("ctx", "fsdp"),
            P("ctx", "fsdp"),
            P("ctx"),
            P(),
            P(),
            P("ctx", None),
            P(None, "fsdp"),
        ),
        out_specs=(
            P("fsdp", "ctx", None),
            P("fsdp", "ctx", None),
            P("fsdp", "ctx", None),
            P("fsdp", "ctx", None),
            P("ctx", None),
            P(None, "fsdp"),
        ),
        check_vma=False,
    )
```

```python
import functools
import math

import jax
import jax.numpy as jnp
from jax import lax
from jax.experimental import pallas as pl
from jax.experimental.pallas import tpu as pltpu
from jax.sharding import PartitionSpec as P

QBLOCK = 64
BOTH = ("fsdp", "ctx")
RING = (0, 3, 1, 2)

normal_levels = (
    -1.0,
    -0.6961928009986877,
    -0.5250730514526367,
    -0.39491748809814453,
    -0.28444138169288635,
    -0.18477343022823334,
    -0.09105003625154495,
    0.0,
    0.07958029955625534,
    0.16093020141124725,
    0.24611230194568634,
    0.33791524171829224,
    0.44070982933044434,
    0.5626170039176941,
    0.7229568362236023,
    1.0,
)
adapter_scale = 0.25


def device_index(x, y, z, c):
    return ((x // 2) * 2 + c) * 32 + y * 8 + z * 2 + x % 2


def ring_pairs(axis0, axis1, step):
    pairs = []
    for x in range(4):
        for y in range(4):
            for z in range(4):
                for c in range(2):
                    to = [x, y, z]
                    axis = (axis0, axis1)[c]
                    to[axis] = (to[axis] + step) % 4
                    pairs.append((device_index(x, y, z, c), device_index(*to, c)))
    return pairs


def send(block, axis0, axis1, step):
    return lax.ppermute(block, BOTH, ring_pairs(axis0, axis1, step))


def swap_cores(block):
    pairs = [
        (device_index(x, y, z, c), device_index(x, y, z, 1 - c))
        for x in range(4)
        for y in range(4)
        for z in range(4)
        for c in range(2)
    ]
    return lax.ppermute(block, BOTH, pairs)


def ring_phase(block, axis0, axis1):
    half = block.shape[0] // 2
    plus = send(block, axis0, axis1, 1)
    minus = send(block, axis0, axis1, -1)
    far_low = send(plus[:half], axis0, axis1, 1)
    far_high = send(minus[half:], axis0, axis1, -1)
    return plus, minus, far_low, far_high


def after(block, *earlier):
    return lax.optimization_barrier((block, earlier))[0]


def along_ctx(shard, by):
    pairs = [(i, i + by) for i in range(32) if 0 <= i + by < 32]
    return lax.ppermute(shard, "ctx", pairs)


def next_rows(block, ctx):
    xl, z = ctx % 2, (ctx // 2) % 4
    along_y = [(i, i + 8) for i in range(32) if i % 8 == 7 and i + 8 < 32]
    relayed = lax.ppermute(block, "ctx", along_y)
    along_z = [
        (i, i + 2 if i % 8 != 7 else i - 6) for i in range(32) if i % 2 == 1 and (i % 8 != 7 or i >= 15)
    ]
    block_z = jnp.where(z == 3, relayed, block)
    relayed = lax.ppermute(block_z, "ctx", along_z)
    return relayed


def pair_rows(block, relayed, ctx):
    crossed = lax.ppermute(
        jnp.where(ctx % 2 == 0, block, relayed), "ctx", [(i, i ^ 1) for i in range(32)]
    )
    return jnp.where(ctx == 0, jnp.zeros_like(crossed), crossed)


def weight_piece(codes, scale_bytes, row_scale, down, up):
    levels = jnp.zeros(codes.shape, jnp.float32)
    for number in range(16):
        levels = jnp.where(codes == number, normal_levels[number], levels)
    absmax = row_scale[:, None] * (scale_bytes.astype(jnp.float32) + 1.0) / 256.0
    absmax = jnp.repeat(absmax, QBLOCK, axis=1)
    weight = (levels * absmax).astype(jnp.bfloat16).astype(jnp.float32)
    low_rank = jnp.dot(down, up, preferred_element_type=jnp.float32)
    return (weight + adapter_scale * low_rank).astype(jnp.bfloat16)


def toeplitz_conv(base, window, width):
    lane = lax.broadcasted_iota(jnp.int32, (128, 2 * width), 1)
    group_of = (lane % width) // 16
    total = None
    for group in range(width // 16):
        row = jnp.broadcast_to(base[group : group + 1, :], (128, 256))
        toep = pltpu.roll(row, 0, 1, stride=1, stride_axis=0).astype(jnp.bfloat16)
        part = jnp.dot(toep, window, preferred_element_type=jnp.float32)
        total = part if total is None else jnp.where(group_of == group, part, total)
    return total


def forward_kernel(base_ref, skip_ref, query_ref, key_ref, value_ref, halo_ref, gated_ref, signal_ref, *, tiles):
    for tile in range(tiles):
        lanes = pl.ds(tile * 128, 128)
        mixed = (
            key_ref[:, lanes].astype(jnp.float32) * value_ref[:, lanes].astype(jnp.float32)
        ).astype(jnp.bfloat16)
        first = jnp.concatenate([halo_ref[:, lanes], mixed[:128]], 0)
        window = jnp.concatenate([first, mixed], 1)
        conv = toeplitz_conv(base_ref[pl.ds(tile * 8, 8), :], window, 128)
        conv = jnp.concatenate([conv[:, :128], conv[:, 128:]], 0)
        gated = conv + skip_ref[:, lanes] * mixed.astype(jnp.float32)
        gated_ref[:, lanes] = gated
        signal_ref[:, lanes] = (query_ref[:, lanes].astype(jnp.float32) * gated).astype(jnp.bfloat16)


def forward_conv(base, skip, query, key, value, halo):
    rows, channels = query.shape
    width = 512
    block = pl.BlockSpec((rows, width), lambda j: (0, j))
    return pl.pallas_call(
        functools.partial(forward_kernel, tiles=width // 128),
        grid=(channels // width,),
        in_specs=[
            pl.BlockSpec((width // 16, 256), lambda j: (j, 0)),
            pl.BlockSpec((1, width), lambda j: (0, j)),
            block,
            block,
            block,
            pl.BlockSpec((128, width), lambda j: (0, j)),
        ],
        out_specs=[block, block],
        out_shape=[
            jax.ShapeDtypeStruct((rows, channels), jnp.float32),
            jax.ShapeDtypeStruct((rows, channels), jnp.bfloat16),
        ],
        compiler_params=pltpu.CompilerParams(vmem_limit_bytes=54 << 20),
        cost_estimate=pl.CostEstimate(flops=1 << 32, bytes_accessed=14 << 20, transcendentals=0),
        name="forward_conv",
    )(base, skip, query, key, value, halo)


def backward_kernel(
    base_ref, skip_ref, head_ref, tail_ref, halo_ref, key_ref, value_ref, *refs, tiles
):
    grad_key_ref, grad_value_ref = refs[-2:]
    for tile in range(tiles):
        lanes = pl.ds(tile * 128, 128)
        here = jnp.concatenate([head_ref[:, lanes], tail_ref[:, lanes]], 0)
        second = jnp.concatenate([tail_ref[:, lanes], halo_ref[:, lanes]], 0)
        window = jnp.concatenate([here, second], 1)
        conv = toeplitz_conv(base_ref[pl.ds(tile * 8, 8), :], window, 128)
        conv = jnp.concatenate([conv[:, :128], conv[:, 128:]], 0)
        mixed = conv + skip_ref[:, lanes] * here.astype(jnp.float32)
        grad_key_ref[:, lanes] = (mixed * value_ref[:, lanes].astype(jnp.float32)).astype(jnp.bfloat16)
        grad_value_ref[:, lanes] = (mixed * key_ref[:, lanes].astype(jnp.float32)).astype(jnp.bfloat16)


def backward_conv(base, skip, head, tail, halo, key, value, part, results):
    rows, channels = key.shape
    width = 512
    skipped = part * (channels // 2 // width)
    block = pl.BlockSpec((rows, width), lambda j: (0, j + skipped))
    half = pl.BlockSpec((128, width), lambda j: (0, j))
    anywhere = pl.BlockSpec(memory_space=pl.ANY)
    return pl.pallas_call(
        functools.partial(backward_kernel, tiles=width // 128),
        grid=(channels // 2 // width,),
        in_specs=[
            pl.BlockSpec((width // 16, 256), lambda j: (j + skipped, 0)),
            pl.BlockSpec((1, width), lambda j: (0, j + skipped)),
            half,
            pl.BlockSpec((128, width), lambda j: (0, j + skipped)),
            half,
            block,
            block,
        ]
        + [anywhere] * len(results),
        out_specs=[block] * 2,
        out_shape=[jax.ShapeDtypeStruct((rows, channels), jnp.bfloat16)] * 2,
        input_output_aliases={7: 0, 8: 1} if results else {},
        compiler_params=pltpu.CompilerParams(vmem_limit_bytes=54 << 20),
        cost_estimate=pl.CostEstimate(flops=1 << 31, bytes_accessed=6 << 20, transcendentals=0),
        name="backward_conv",
    )(base, skip, head, tail, halo, key, value, *results)


def project_kernel(*refs, groups, first, last):
    refs = list(refs)
    meta = refs.pop(0)
    signal_ref, cot_ref = refs.pop(0), refs.pop(0)
    if not first:
        out_in, back_in = refs.pop(0), refs.pop(0)
    arrays = [[refs.pop(0) for _ in range(count)] for _, _, count in groups]
    if last:
        gated_ref, query_ref, out_ref, grad_query_ref, *head_refs = refs[:6]
        tail_ref, refs = refs[6], refs[7:]
    else:
        out_ref, back_ref = refs[:2]
        refs = refs[2:]
    signal, picked, cot, out_acc, back_acc, held, sems, io_sems = refs[:8]
    x0, y0, z0, core = meta[0], meta[1], meta[2], meta[3]
    rows = signal.shape[0]
    loads = [
        pltpu.make_async_copy(signal_ref, signal, io_sems.at[0]),
        pltpu.make_async_copy(cot_ref, cot, io_sems.at[1]),
    ]
    if not first:
        loads.append(pltpu.make_async_copy(out_in, out_acc, io_sems.at[3]))
        loads.append(pltpu.make_async_copy(back_in, back_acc, io_sems.at[4]))
    for load in loads:
        load.start()
    copies = []
    for g, (mine, _, count) in enumerate(groups):
        chain = core if mine else 1 - core
        each = 16 // count
        group = []
        for n in range(16):
            a, b = RING[n // 4], RING[n % 4]
            x = (x0 + jnp.where(chain == 0, b, a)) & 3
            w = jnp.where(chain == 0, y0 + a, z0 + b) & 3
            slot = pl.multiple_of(((x >> 1) * 8 + w * 2 + (x & 1)) * 128, 128)
            source = arrays[g][n // each].at[pl.ds((n % each) * 128, 128), :]
            group.append(
                pltpu.make_async_copy(source, held.at[g, pl.ds(slot, 128), :], sems.at[g, n])
            )
        copies.append(group)
    for group in copies[:2]:
        for copy in group:
            copy.start()
    late = []
    if last:
        gated, query, gradient = refs[8:11]
        for n, (source, target) in enumerate([(gated_ref, gated), (query_ref, query)]):
            late.append(pltpu.make_async_copy(source, target, io_sems.at[5 + n]))
    if first:
        out_acc[...] = jnp.zeros_like(out_acc)
        back_acc[...] = jnp.zeros_like(back_acc)
    for load in loads:
        load.wait()
    for g, (mine, offset, _) in enumerate(groups):
        chain = core if mine else 1 - core
        fixed = jnp.where(chain == 0, z0 + offset, y0 + offset) & 3

        def channels(w, chain=chain, fixed=fixed):
            return pl.multiple_of(jnp.where(chain == 0, w * 4 + fixed, fixed * 4 + w) * 256, 256)

        for w in range(4):
            picked[:, w * 256 : (w + 1) * 256] = signal[:, pl.ds(channels(w), 256)]
        for copy in copies[g]:
            copy.wait()
        for copy in copies[g + 2] if g + 2 < len(groups) else late if g == 0 else ():
            copy.start()

        @pl.loop(0, 2)
        def _(xh, g=g, chain=chain, channels=channels):
            cols = pl.ds(pl.multiple_of((xh * 2 + chain) * 1024, 1024), 1024)
            weight = held.at[g, pl.ds(pl.multiple_of(xh * 1024, 1024), 1024), :]
            out_acc[:, cols] += jnp.dot(picked[...], weight[...], preferred_element_type=jnp.float32)
            back = lax.dot_general(
                cot[:, cols], weight[...], (((1,), (1,)), ((), ())), preferred_element_type=jnp.float32
            )
            for w in range(4):
                back_acc[:, pl.ds(channels(w), 256)] += back[:, w * 256 : (w + 1) * 256]

    if not last:
        stores = [
            pltpu.make_async_copy(out_acc, out_ref, io_sems.at[0]),
            pltpu.make_async_copy(back_acc, back_ref, io_sems.at[1]),
        ]
        for store in stores:
            store.start()
        for store in stores:
            store.wait()
        return
    signal[...] = out_acc[...].astype(jnp.bfloat16)
    stores = [pltpu.make_async_copy(signal, out_ref, io_sems.at[0])]
    stores[0].start()
    for load in late:
        load.wait()
    for quarter in range(4):

        @pl.loop(0, 4)
        def _(step, quarter=quarter):
            lanes = pl.ds(pl.multiple_of(quarter * 1024 + step * 256, 256), 256)
            back = back_acc[:, lanes]
            gradient[:, lanes] = (back * query[:, lanes].astype(jnp.float32)).astype(jnp.bfloat16)
            query[:, lanes] = (back * gated[:, lanes]).astype(jnp.bfloat16)

        part = pl.ds(quarter * 1024, 1024)
        head = head_refs[quarter // 2].at[:, pl.ds((quarter % 2) * 1024, 1024)]
        for n, (source, target) in enumerate(
            [
                (gradient.at[pl.ds(0, 128), part], head),
                (gradient.at[pl.ds(128, 128), part], tail_ref.at[:, part]),
                (query.at[:, part], grad_query_ref.at[:, part]),
            ]
        ):
            stores.append(pltpu.make_async_copy(source, target, sems.at[0, quarter * 3 + n]))
            stores[-1].start()
    for store in stores:
        store.wait()


def project(meta, signal, cot, sums, groups, finish=None):
    rows, channels = signal.shape
    first, last = sums is None, finish is not None
    arrays = [array for group in groups for array in group[2]]
    static = tuple((mine, offset, len(held)) for mine, offset, held in groups)
    anywhere = pl.BlockSpec(memory_space=pl.ANY)
    operands = [meta, signal, cot] + ([] if first else list(sums)) + arrays
    in_specs = [pl.BlockSpec(memory_space=pltpu.SMEM)] + [anywhere] * (len(operands) - 1)
    flops = len(groups) * 16 * 128 * 1024 * 2 * rows * 2
    moved = len(groups) * (4 << 20) + (16 << 20)
    scratch = [
        pltpu.VMEM((rows, channels), jnp.bfloat16),
        pltpu.VMEM((rows, 1024), jnp.bfloat16),
        pltpu.VMEM((rows, channels), jnp.bfloat16),
        pltpu.VMEM((rows, channels), jnp.float32),
        pltpu.VMEM((rows, channels), jnp.float32),
        pltpu.VMEM((len(groups), 2048, 1024), jnp.bfloat16),
        pltpu.SemaphoreType.DMA((len(groups), 16)),
        pltpu.SemaphoreType.DMA((10,)),
    ]
    if last:
        operands += list(finish)
        in_specs += [anywhere] * 2
        out_shape = [jax.ShapeDtypeStruct((rows, channels), jnp.bfloat16)] * 2
        out_shape += [jax.ShapeDtypeStruct((128, channels // 2), jnp.bfloat16)] * 2
        out_shape += [jax.ShapeDtypeStruct((128, channels), jnp.bfloat16)]
        scratch += [
            pltpu.VMEM((rows, channels), jnp.float32),
            pltpu.VMEM((rows, channels), jnp.bfloat16),
            pltpu.VMEM((rows, channels), jnp.bfloat16),
        ]
        aliases = {}
    else:
        out_shape = [
            jax.ShapeDtypeStruct((rows, channels), jnp.float32),
            jax.ShapeDtypeStruct((rows, channels), jnp.float32),
        ]
        aliases = {} if first else {3: 0, 4: 1}
    return pl.pallas_call(
        functools.partial(project_kernel, groups=static, first=first, last=last),
        in_specs=in_specs,
        out_specs=[anywhere] * len(out_shape),
        out_shape=out_shape,
        scratch_shapes=scratch,
        input_output_aliases=aliases,
        compiler_params=pltpu.CompilerParams(vmem_limit_bytes=54 << 20),
        cost_estimate=pl.CostEstimate(flops=flops, bytes_accessed=moved, transcendentals=0),
        name="project",
    )(*operands)


def gathered_adapters(down_piece, up_piece, ctx, fsdp):
    quarter = lax.dynamic_slice_in_dim(down_piece.T, fsdp * 16, 16, 0)
    block = lax.dynamic_slice(up_piece, ((ctx // 4) * 8, (ctx % 4) * 256), (8, 256))
    block = jnp.concatenate([block[:, :128], block[:, 128:]], 0)
    share = jnp.concatenate([quarter, block], 0)
    shares = lax.all_to_all(jnp.broadcast_to(share[None], (128, 32, 128)), BOTH, 0, 0, tiled=True)
    return shares


def adapter_kernel(signal_ref, cot_ref, shares_ref, parts_ref, down_ref, up_ref):
    for d in range(128):
        fsdp, ctx = d // 32, d % 32
        down_ref[fsdp * 16 : fsdp * 16 + 16, ctx * 128 : ctx * 128 + 128] = shares_ref[d, 0:16, :]
        top, left = (ctx // 4) * 8, fsdp * 1024 + (ctx % 4) * 256
        up_ref[top : top + 8, left : left + 128] = shares_ref[d, 16:24, :]
        up_ref[top : top + 8, left + 128 : left + 256] = shares_ref[d, 24:32, :]
    across = (((1,), (1,)), ((), ()))
    over_rows = (((0,), (0,)), ((), ()))
    down_projection = lax.dot_general(
        signal_ref[...], down_ref[...], across, preferred_element_type=jnp.float32
    ).astype(jnp.bfloat16)
    back_up = lax.dot_general(
        cot_ref[...], up_ref[...], across, preferred_element_type=jnp.float32
    ).astype(jnp.bfloat16)
    down_ref[...] = lax.dot_general(
        back_up, signal_ref[...], over_rows, preferred_element_type=jnp.float32
    ).astype(jnp.bfloat16)
    up_ref[...] = lax.dot_general(
        down_projection, cot_ref[...], over_rows, preferred_element_type=jnp.float32
    ).astype(jnp.bfloat16)
    for d in range(128):
        fsdp, ctx = d // 32, d % 32
        parts_ref[d, 0:16, :] = down_ref[fsdp * 16 : fsdp * 16 + 16, ctx * 128 : ctx * 128 + 128]
        top, left = (ctx // 4) * 8, fsdp * 1024 + (ctx % 4) * 256
        parts_ref[d, 16:24, :] = up_ref[top : top + 8, left : left + 128]
        parts_ref[d, 24:32, :] = up_ref[top : top + 8, left + 128 : left + 256]


def adapter_terms(signal, cot, shares):
    return pl.pallas_call(
        adapter_kernel,
        out_shape=jax.ShapeDtypeStruct((128, 32, 128), jnp.bfloat16),
        scratch_shapes=[pltpu.VMEM((64, 4096), jnp.bfloat16)] * 2,
        compiler_params=pltpu.CompilerParams(vmem_limit_bytes=54 << 20),
        cost_estimate=pl.CostEstimate(flops=1 << 32, bytes_accessed=6 << 20, transcendentals=0),
        name="adapter_terms",
    )(signal, cot, shares)


def adapter_sums(parts, multiplier):
    sums = (multiplier * jnp.sum(parts.astype(jnp.float32), 0)).astype(jnp.bfloat16)
    mine = sums[:16]
    others = [lax.ppermute(mine, "fsdp", [(i, i ^ k) for i in range(4)]) for k in (1, 2, 3)]
    up = lax.all_to_all(jnp.broadcast_to(sums[None, 16:], (32, 16, 128)), "ctx", 0, 0, tiled=True)
    return [mine] + others, up


def adapter_down(blocks, fsdp):
    odd, high = fsdp % 2 == 1, fsdp // 2 == 1
    blocks = [jnp.where(odd, blocks[k ^ 1], blocks[k]) for k in range(4)]
    blocks = [jnp.where(high, blocks[k ^ 2], blocks[k]) for k in range(4)]
    return jnp.concatenate(blocks, 0).T


def adapter_up(up):
    return jnp.transpose(up.reshape(8, 4, 2, 8, 128), (0, 3, 1, 2, 4)).reshape(64, 1024)


def local(
    query_branch,
    key_branch,
    value_branch,
    cotangent,
    quantized_weight_codes,
    scale_code_bytes,
    row_scale_second,
    filters,
    channel_skip_weight,
    adapter_down_weight,
    adapter_up_weight,
):
    query, key, value, cot = query_branch[0], key_branch[0], value_branch[0], cotangent[0]
    rows, channels = query.shape
    multiplier = adapter_scale / math.sqrt(4 * 8192)
    ctx, fsdp = lax.axis_index("ctx"), lax.axis_index("fsdp")
    core = fsdp % 2
    meta = jnp.stack([(fsdp // 2) * 2 + ctx % 2, ctx // 8, (ctx // 2) % 4, core]).astype(jnp.int32)

    piece = weight_piece(
        quantized_weight_codes, scale_code_bytes, row_scale_second, adapter_down_weight, adapter_up_weight
    )
    mixed_tail = (key[128:].astype(jnp.float32) * value[128:].astype(jnp.float32)).astype(jnp.bfloat16)
    relayed = next_rows(mixed_tail, ctx)
    plus, minus, low, high = ring_phase(piece, 0, 2)
    held = jnp.concatenate([piece, plus, minus, low, high], 0)
    shares = gathered_adapters(after(adapter_down_weight, held), adapter_up_weight, ctx, fsdp)
    plus, minus, low, high = ring_phase(held, 1, 0)
    front = jnp.concatenate([held, plus], 0)
    rear = after(jnp.concatenate([minus, low, high], 0), front, relayed, shares)
    mixed_halo = pair_rows(mixed_tail, after(relayed, rear), ctx)
    plus_front, minus_front = send(front, 2, 1, 1), send(front, 2, 1, -1)
    plus_rear, minus_rear = send(rear, 2, 1, 1), send(rear, 2, 1, -1)

    taps = filters.astype(jnp.float32)
    forward_base = jnp.pad(jnp.flip(taps, 1), ((0, 0), (1, 127)))
    backward_base = jnp.pad(taps, ((0, 0), (0, 128)))
    skip = channel_skip_weight[None]
    gated, signal = forward_conv(forward_base, skip, query, key, after(value, rear), mixed_halo)

    far_front = send(after(plus_front, signal), 2, 1, 1)
    far_rear = send(minus_rear, 2, 1, -1)
    terms = adapter_terms(after(signal, plus_front), cot, shares)
    parts = lax.all_to_all(terms, BOTH, 0, 0, tiled=True)
    swapped = [swap_cores(after(block, signal)) for block in (front, rear)]
    swapped += [
        swap_cores(after(block, terms)) for block in (plus_front, plus_rear, minus_front, minus_rear)
    ]
    sums = project(
        meta,
        after(signal, terms),
        cot,
        None,
        [
            (True, 0, [front, rear]),
            (False, 0, swapped[:2]),
            (True, -1, [plus_front, plus_rear]),
            (False, -1, swapped[2:4]),
            (True, 1, [minus_front, minus_rear]),
            (False, 1, swapped[4:]),
        ],
    )
    far = [swap_cores(after(block, sums[0])) for block in (far_front, far_rear)]
    output, grad_query, head_a, head_b, tail = project(
        meta,
        signal,
        cot,
        sums,
        [(True, 2, [far_front, far_rear]), (False, 2, far)],
        (gated, query),
    )
    halo_a, halo_b = along_ctx(head_a, -1), along_ctx(head_b, -1)
    down_blocks, up_blocks = adapter_sums(after(parts, output), multiplier)
    results = backward_conv(backward_base, skip, head_a, tail, halo_a, key, value, 0, ())
    grad_key, grad_value = backward_conv(
        backward_base, skip, head_b, tail, halo_b, key, value, 1, tuple(results)
    )
    grad_up = adapter_up(after(up_blocks, grad_key))
    grad_down = adapter_down(after(down_blocks, grad_key), fsdp)
    return output[None], grad_query[None], grad_key[None], grad_value[None], grad_down, grad_up


def solution(mesh):
    return jax.shard_map(
        local,
        mesh=mesh,
        in_specs=(
            P("fsdp", "ctx", None),
            P("fsdp", "ctx", None),
            P("fsdp", "ctx", None),
            P("fsdp", "ctx", None),
            P("ctx", "fsdp"),
            P("ctx", "fsdp"),
            P("ctx"),
            P(),
            P(),
            P("ctx", None),
            P(None, "fsdp"),
        ),
        out_specs=(
            P("fsdp", "ctx", None),
            P("fsdp", "ctx", None),
            P("fsdp", "ctx", None),
            P("fsdp", "ctx", None),
            P("ctx", None),
            P(None, "fsdp"),
        ),
        check_vma=False,
    )
```
